32 devices in a mesh: dp: 16 (over z, x, core), fsdp: 2 (over y).
Axes of the slice: x: 2, y: 2, z: 4, core: 2. Of those that a mesh axis runs over, the one named last changes fastest.
Arguments:
- tokens: bfloat16 [16384, 768], P(('dp', 'fsdp')), may hold values from -6 to 6
- cotangent: bfloat16 [16384, 768], P(('dp', 'fsdp')), may hold values from -6 to 6
- segments: int32 [32, 512], P(('dp', 'fsdp')), may hold values from 0 to 7, never falling along the last dimension, each value on 1 to 256 neighbouring positions
- bucket_line: int32 [32, 512, 512], P(('dp', 'fsdp')), may hold values from 0 to 31
- bucket_plane: int32 [32, 512, 512], P(('dp', 'fsdp')), may hold values from 0 to 31
- query_weight: bfloat16 [768, 768], P('fsdp'), may hold values from -0.21875 to 0.21875
- query_bias: bfloat16 [768], P('fsdp'), may hold values from -1.75 to 1.75
- key_weight: bfloat16 [768, 768], P('fsdp'), may hold values from -0.21875 to 0.21875
- value_weight: bfloat16 [768, 768], P('fsdp'), may hold values from -0.21875 to 0.21875
- value_bias: bfloat16 [768], P('fsdp'), may hold values from -1.75 to 1.75
- output_weight: bfloat16 [768, 768], P('fsdp'), may hold values from -0.875 to 0.875
- output_bias: bfloat16 [768], P('fsdp'), may hold values from -1.75 to 1.75
- attn_gain: bfloat16 [768], P('fsdp'), may hold values from 0.25 to 1.75
- attn_shift: bfloat16 [768], P('fsdp'), may hold values from -1.75 to 1.75
- inner_weight: bfloat16 [768, 3072], P('fsdp'), may hold values from -0.21875 to 0.21875
- inner_bias: bfloat16 [3072], P('fsdp'), may hold values from -1.75 to 1.75
- outer_weight: bfloat16 [3072, 768], P('fsdp'), may hold values from -0.109375 to 0.109375
- outer_bias: bfloat16 [768], P('fsdp'), may hold values from -1.75 to 1.75
- ffn_gain: bfloat16 [768], P('fsdp'), may hold values from 0.25 to 1.75
- ffn_shift: bfloat16 [768], P('fsdp'), may hold values from -1.75 to 1.75
- line_table: bfloat16 [32, 12], P('fsdp'), may hold values from -6 to 6
- plane_table: bfloat16 [32, 12], P('fsdp'), may hold values from -6 to 6
Outputs:
- layer_out: bfloat16 [16384, 768], P(('dp', 'fsdp'))
- input_grad: float32 [16384, 768], P(('dp', 'fsdp'))
- grad_query_weight: float32 [768, 768], P('fsdp')
- grad_query_bias: float32 [768], P('fsdp')
- grad_key_weight: float32 [768, 768], P('fsdp')
- grad_value_weight: float32 [768, 768], P('fsdp')
- grad_value_bias: float32 [768], P('fsdp')
- grad_output_weight: float32 [768, 768], P('fsdp')
- grad_output_bias: float32 [768], P('fsdp')
- grad_attn_gain: float32 [768], P('fsdp')
- grad_attn_shift: float32 [768], P('fsdp')
- grad_inner_weight: float32 [768, 3072], P('fsdp')
- grad_inner_bias: float32 [3072], P('fsdp')
- grad_outer_weight: float32 [3072, 768], P('fsdp')
- grad_outer_bias: float32 [768], P('fsdp')
- grad_ffn_gain: float32 [768], P('fsdp')
- grad_ffn_shift: float32 [768], P('fsdp')
- grad_line_table: float32 [32, 12], P('fsdp')
- grad_plane_table: float32 [32, 12], P('fsdp')
The draws below stay inside these ranges and needn't reach their ends.
Inputs may be any that keep to these rules, and one draw needn't show every extreme that they name: `segments`: within each window the document numbers never fall; each document holds 1 to 256 tokens.
All inputs are finite; a program needn't handle non-finite values.
Results may differ from the reference program's by a relative error of at most 0.013.
Values may be sent and summed in bfloat16 or wider, within the bound.
No kernel may reach another device: no remote copies, remote signals or barrier semaphores. Data moves between devices by JAX's collectives and lax.ppermute only.
A program may use at most 192 MiB of HBM per device.

```python
import math
import jax
import jax.numpy as jnp
import numpy as np
from jax import lax

D = 768
HEADS = 12
FF = 3072
BUCKETS = 32
SEQ = 512
WINDOWS = 32
TOKENS = 16384


def place_ends(values, stream_key, smallest, high):
    dims = values.shape
    place = [jax.random.randint(jax.random.fold_in(stream_key, axis), (), 0, dims[axis]) for axis in range(len(dims))]
    values = values.at[tuple(place)].set(smallest)
    longest = dims.index(max(dims))
    place[longest] = (place[longest] + 1) % dims[longest]
    return values.at[tuple(place)].set(high)


def block_levels(stream_key, dims, cuts, least, high):
    level = 1.0
    for axis_at, blocks in cuts:
        draws = jax.random.uniform(jax.random.fold_in(jax.random.fold_in(stream_key, 6), axis_at), (blocks,), jnp.float32, least / len(cuts), high / len(cuts))
        level = level * jnp.repeat(jnp.exp(draws), dims[axis_at] // blocks).reshape((-1,) + (1,) * (len(dims) - 1 - axis_at))
    return level


def length_profile(count, total, bound, slope):
    weights = [(1 << 20) // math.isqrt(standing ** slope) + 1 for standing in range(2, count + 1)]
    rest, counts = total - bound - (count - 1), [1] * (count - 1)
    while rest > 0:
        movable = [i for i in range(count - 1) if counts[i] < bound]
        mass, left = sum([weights[i] for i in movable]), rest
        for i in movable:
            more = min(bound - counts[i], max(1, left * weights[i] // mass), rest)
            counts[i] = counts[i] + more
            rest = rest - more
    return np.array([bound] + counts)


def ragged(stream_key, number_of, total, bound, skew):
    if number_of == 2:
        one = jax.random.randint(stream_key, (), max(1, total - bound), min(bound, total - 1) + 1)
        return jnp.stack([one, total - one])
    sizes = jnp.asarray(length_profile(number_of, total, bound, skew), jnp.int32)
    couples = (number_of - 1) // 2
    source_of, taker = sizes[1:1 + 2 * couples:2], sizes[2:2 + 2 * couples:2]
    slack = jnp.minimum(source_of - 1, bound - taker)
    shifted = jax.random.randint(jax.random.fold_in(stream_key, 1), (couples,), 0, 1 << 20) % (slack + 1)
    sizes = sizes.at[1:1 + 2 * couples:2].set(source_of - shifted).at[2:2 + 2 * couples:2].set(taker + shifted)
    return sizes[jax.random.permutation(jax.random.fold_in(stream_key, 2), number_of)]


def centred(key, shape, scale, limit, cuts=(), held_as=jnp.bfloat16):
    factor_of = block_levels(key, shape, cuts, -0.22, 0.18) if cuts else 1.0
    entries = jax.random.normal(key, shape, jnp.float32) * scale * factor_of
    return jnp.minimum(jnp.maximum(entries, -limit), limit).astype(held_as)


def setup_inputs(seed: int = 0) -> dict:
    arg_keys = jax.random.split(jax.random.key(seed), 23)
    return {
        "tokens": centred(arg_keys[0], (TOKENS, D), 1.0, 6.0, ((0, 32),)),
        "cotangent": centred(arg_keys[1], (TOKENS, D), 1.0, 6.0, ((0, 32),)),
        "segments": jax.vmap(lambda own: jnp.searchsorted(jnp.cumsum(ragged(own, max(SEQ // 64, 4), SEQ, SEQ // 2, 2)), jnp.arange(SEQ), side="right"))(jax.random.split(arg_keys[2], WINDOWS)).reshape((WINDOWS, SEQ)).astype(jnp.int32),
        "bucket_line": place_ends(jax.random.randint(arg_keys[3], (WINDOWS, SEQ, SEQ), 0, BUCKETS), jax.random.fold_in(arg_keys[3], 1), 0, BUCKETS - 1).astype(jnp.int32),
        "bucket_plane": place_ends(jax.random.randint(arg_keys[4], (WINDOWS, SEQ, SEQ), 0, BUCKETS), jax.random.fold_in(arg_keys[4], 1), 0, BUCKETS - 1).astype(jnp.int32),
        "query_weight": centred(arg_keys[5], (D, D), D ** -0.5, 0.21875, ((0, 2),)),
        "query_bias": centred(arg_keys[6], (D,), 0.3, 1.75, ((0, 2),)),
        "key_weight": centred(arg_keys[7], (D, D), D ** -0.5, 0.21875, ((0, 2),)),
        "value_weight": centred(arg_keys[8], (D, D), D ** -0.5, 0.21875, ((0, 2),)),
        "value_bias": centred(arg_keys[9], (D,), 0.3, 1.75, ((0, 2),)),
        "output_weight": centred(arg_keys[10], (D, D), (D // 16) ** -0.5, 0.875, ((0, 2),)),
        "output_bias": centred(arg_keys[11], (D,), 0.3, 1.75, ((0, 2),)),
        "attn_gain": jnp.clip(1.0 + 0.15 * jax.random.normal(arg_keys[12], (D,), jnp.float32), 0.25, 1.75).astype(jnp.bfloat16),
        "attn_shift": centred(arg_keys[13], (D,), 0.3, 1.75, ((0, 2),)),
        "inner_weight": centred(arg_keys[14], (D, FF), D ** -0.5, 0.21875, ((0, 2),)),
        "inner_bias": centred(arg_keys[15], (FF,), 0.3, 1.75, ((0, 2),)),
        "outer_weight": centred(arg_keys[16], (FF, D), FF ** -0.5, 0.109375, ((0, 2),)),
        "outer_bias": centred(arg_keys[17], (D,), 0.3, 1.75, ((0, 2),)),
        "ffn_gain": jnp.clip(1.0 + 0.15 * jax.random.normal(arg_keys[18], (D,), jnp.float32), 0.25, 1.75).astype(jnp.bfloat16),
        "ffn_shift": centred(arg_keys[19], (D,), 0.3, 1.75, ((0, 2),)),
        "line_table": centred(arg_keys[20], (BUCKETS, HEADS), 1.0, 6.0, ((0, 2),)),
        "plane_table": centred(arg_keys[21], (BUCKETS, HEADS), 1.0, 6.0, ((0, 2),)),
    }


@jax.custom_vjp
def low(v):
    return lax.optimization_barrier(v.astype(jnp.bfloat16)).astype(jnp.float32)

@jax.custom_vjp
def low_back(v):
    return v

def low_keep(v):
    return (low(v), None)

def low_pass(kept, grad):
    return (grad,)

def back_keep(v):
    return (v, None)

def back_low(kept, grad):
    return (low(grad),)
low.defvjp(low_keep, low_pass)
low_back.defvjp(back_keep, back_low)
masked_score = -1000000000.0
norm_epsilon = 1e-05

def product(former, latter):
    return jnp.dot(former, latter, precision=lax.Precision.HIGHEST, preferred_element_type=jnp.float32)

def layer_norm(values, gain, shift):
    center = values - lax.optimization_barrier(jnp.mean(values, -1, keepdims=True))
    spread = lax.optimization_barrier(jnp.mean(center * center, -1, keepdims=True))
    return center * lax.rsqrt(spread + norm_epsilon) * gain + shift

def window_attention(query, keys, values, segment, line, plane, line_table, plane_table):
    bias = jnp.transpose(line_table[line] + plane_table[plane], (2, 0, 1))
    scores = jnp.einsum('qhe,khe->hqk', query, keys, precision=lax.Precision.HIGHEST) + bias
    scores = low_back(scores)
    same = segment[:, None] == segment[None, :]
    scores = jnp.where(same[None], scores, masked_score)
    row_max = lax.optimization_barrier(jnp.max(scores, -1, keepdims=True))
    expd = jnp.exp(scores - row_max)
    weights = low(expd / lax.optimization_barrier(jnp.sum(expd, -1, keepdims=True)))
    return jnp.einsum('hqk,khe->qhe', weights, values, precision=lax.Precision.HIGHEST)

def forward_block(inputs, params, segment, line, plane):
    query_weight, query_bias, key_weight, value_weight, value_bias, output_weight, output_bias, attn_gain, attn_shift, inner_weight, inner_bias, outer_weight, outer_bias, ffn_gain, ffn_shift, line_table, plane_table = params
    windows, length = segment.shape
    head_count = line_table.shape[1]
    features = inputs.shape[1]

    def split_heads(tensor):
        return tensor.reshape(windows, length, head_count, features // head_count)
    query = low_back(low((product(inputs, query_weight) + query_bias) * 0.125))
    keys = low_back(low(product(inputs, key_weight)))
    values = low_back(low(product(inputs, value_weight) + value_bias))
    attend = jax.checkpoint(window_attention)
    context = lax.map(lambda pieces: attend(pieces[0], pieces[1], pieces[2], pieces[3], pieces[4], pieces[5], line_table, plane_table), (split_heads(query), split_heads(keys), split_heads(values), segment, line, plane))
    context = low_back(low(context.reshape(windows * length, features)))
    attended = low_back(product(context, output_weight) + output_bias)
    first = layer_norm(inputs + attended, attn_gain, attn_shift)
    inner = low_back(product(low(first), inner_weight) + inner_bias)
    activated = low(jax.nn.gelu(inner, approximate=False))
    outer = low_back(product(activated, outer_weight) + outer_bias)
    return layer_norm(first + outer, ffn_gain, ffn_shift)

def reference(tokens, cotangent, segments, bucket_line, bucket_plane, query_weight, query_bias, key_weight, value_weight, value_bias, output_weight, output_bias, attn_gain, attn_shift, inner_weight, inner_bias, outer_weight, outer_bias, ffn_gain, ffn_shift, line_table, plane_table):
    params = tuple((weight.astype(jnp.float32) for weight in (query_weight, query_bias, key_weight, value_weight, value_bias, output_weight, output_bias, attn_gain, attn_shift, inner_weight, inner_bias, outer_weight, outer_bias, ffn_gain, ffn_shift, line_table, plane_table)))
    per_group = 8
    length = segments.shape[1]
    features = tokens.shape[1]
    group_count = segments.shape[0] // per_group
    inputs = tokens.astype(jnp.float32).reshape(group_count, per_group * length, features)
    cotans = cotangent.astype(jnp.float32).reshape(group_count, per_group * length, features)
    seg_groups = segments.reshape(group_count, per_group, length)
    line_groups = bucket_line.reshape(group_count, per_group, length, length)
    plane_groups = bucket_plane.reshape(group_count, per_group, length, length)

    def step(carry, pieces):
        block_in, block_cot, segment, line, plane = pieces
        result, pull = jax.vjp(lambda source, weights: forward_block(source, weights, segment, line, plane), block_in, params)
        grad_in, grad_params = pull(block_cot)
        carry = tuple((total + grad for total, grad in zip(carry, grad_params)))
        return (carry, (result.astype(jnp.bfloat16), grad_in))
    start = tuple((jnp.zeros_like(weight) for weight in params))
    totals, (results, grads_in) = lax.scan(step, start, (inputs, cotans, seg_groups, line_groups, plane_groups))
    layer_out = results.reshape(-1, features)
    input_grad = grads_in.reshape(-1, features)
    return (layer_out, input_grad, totals[0], totals[1], totals[2], totals[3], totals[4], totals[5], totals[6], totals[7], totals[8], totals[9], totals[10], totals[11], totals[12], totals[13], totals[14], totals[15], totals[16])
```

```python
from functools import partial

import jax
import jax.numpy as jnp
from jax import lax
from jax.experimental import pallas as pl
from jax.experimental.pallas import tpu as pltpu
from jax.sharding import PartitionSpec as P

masked_score = -1000000000.0
norm_epsilon = 1e-05


def matmul(former, latter):
    return jnp.dot(former, latter, preferred_element_type=jnp.float32)


def rows_product(former, latter):
    return lax.dot_general(
        former, latter, (((0,), (0,)), ((), ())), preferred_element_type=jnp.float32
    )


def back_product(former, latter):
    return lax.dot_general(
        former, latter, (((1,), (1,)), ((), ())), preferred_element_type=jnp.float32
    )


def layer_norm(values, gain, shift):
    center = values - jnp.mean(values, -1, keepdims=True)
    spread = jnp.mean(center * center, -1, keepdims=True)
    return center * lax.rsqrt(spread + norm_epsilon) * gain + shift


def bucket_hits(bucket_rows, bucket_count):
    labels = lax.broadcasted_iota(jnp.int32, (bucket_count, 1), 0)
    return (bucket_rows.reshape(1, -1) == labels).astype(jnp.bfloat16)


def pair_bias(line_heads, plane_heads, line_rows, plane_rows):
    bucket_count = line_heads.shape[1]
    total = matmul(line_heads, bucket_hits(line_rows, bucket_count))
    total = total + matmul(plane_heads, bucket_hits(plane_rows, bucket_count))
    return total.reshape(line_heads.shape[0], line_rows.shape[0], line_rows.shape[1])


def pair_grad(dscore_rows, line_rows, plane_rows, bucket_count):
    flat_grad = dscore_rows.reshape(dscore_rows.shape[0], -1)
    return (
        back_product(flat_grad, bucket_hits(line_rows, bucket_count)),
        back_product(flat_grad, bucket_hits(plane_rows, bucket_count)),
    )


def window_scores(line_heads, plane_heads, query, keys, segment, line_win, plane_win):
    length, features = keys.shape
    head_count = line_heads.shape[0]
    head_dim = features // head_count
    row_block = min(length, 128)
    block_count = length // row_block
    line_blocks = line_win.reshape(block_count, row_block, length)
    plane_blocks = plane_win.reshape(block_count, row_block, length)
    bias = lax.map(
        lambda pieces: pair_bias(line_heads, plane_heads, pieces[0], pieces[1]),
        (line_blocks, plane_blocks),
    )
    query_heads = query.reshape(block_count, row_block, head_count, head_dim)
    key_heads = keys.reshape(length, head_count, head_dim)
    scores = (
        jnp.einsum("nrhe,khe->nhrk", query_heads, key_heads, preferred_element_type=jnp.float32)
        + bias
    )
    same = segment.reshape(block_count, 1, row_block, 1) == segment.reshape(1, 1, 1, length)
    return (
        jnp.where(same, scores, masked_score),
        query_heads,
        key_heads,
        line_blocks,
        plane_blocks,
    )


def window_forward(line_heads, plane_heads, pieces):
    query, keys, values, segment, line_win, plane_win = pieces
    length, features = keys.shape
    head_count = line_heads.shape[0]
    scores, query_heads, key_heads, line_blocks, plane_blocks = window_scores(
        line_heads, plane_heads, query, keys, segment, line_win, plane_win
    )
    row_max = jnp.max(scores, -1, keepdims=True)
    expd = jnp.exp(scores - row_max)
    total = jnp.sum(expd, -1, keepdims=True)
    log_total = row_max + jnp.log(total)
    weights = (expd / total).astype(jnp.bfloat16)
    value_heads = values.reshape(length, head_count, features // head_count)
    context = jnp.einsum("nhrk,khe->nrhe", weights, value_heads, preferred_element_type=jnp.float32)
    return (context.reshape(length, features), log_total)


def window_backward(line_heads, plane_heads, pieces):
    query, keys, values, segment, line_win, plane_win, log_total, dcontext = pieces
    length, features = keys.shape
    head_count = line_heads.shape[0]
    bucket_count = line_heads.shape[1]
    scores, query_heads, key_heads, line_blocks, plane_blocks = window_scores(
        line_heads, plane_heads, query, keys, segment, line_win, plane_win
    )
    probs = jnp.exp(scores - log_total)
    weights = probs.astype(jnp.bfloat16)
    value_heads = values.reshape(length, head_count, features // head_count)
    dcontext_heads = dcontext.reshape(query_heads.shape)
    dprobs = jnp.einsum(
        "nrhe,khe->nhrk", dcontext_heads, value_heads, preferred_element_type=jnp.float32
    )
    row_inner = jnp.sum(probs * dprobs, -1, keepdims=True)
    dscores = (probs * (dprobs - row_inner)).astype(jnp.bfloat16)
    dquery = jnp.einsum("nhrk,khe->nrhe", dscores, key_heads, preferred_element_type=jnp.float32)
    dkeys = jnp.einsum("nhrk,nrhe->khe", dscores, query_heads, preferred_element_type=jnp.float32)
    dvalues = jnp.einsum(
        "nhrk,nrhe->khe", weights, dcontext_heads, preferred_element_type=jnp.float32
    )
    line_grad, plane_grad = lax.map(
        lambda parts: pair_grad(parts[0], parts[1], parts[2], bucket_count),
        (dscores, line_blocks, plane_blocks),
    )
    return (
        dquery.reshape(length, features),
        dkeys.reshape(length, features),
        dvalues.reshape(length, features),
        jnp.sum(line_grad, 0),
        jnp.sum(plane_grad, 0),
    )


def bits_of(count):
    return count.bit_length() - 1


def swap(value, axis, count, bit):
    return lax.ppermute(value, axis, [(i, i ^ (1 << bit)) for i in range(count)])


def place_kernel(starts, rows_at, columns_at, *refs):
    sources, out_ref = refs[:-1], refs[-1]
    step = pl.program_id(0)
    for source, start, stop in zip(sources, starts[:-1], starts[1:]):

        @pl.when(jnp.logical_and(step >= start, step < stop))
        def _(source=source):
            out_ref[...] = source[...].astype(out_ref.dtype)


def place(pieces, row_blocks, column_blocks, dtype):
    starts, rows_at, columns_at = [0], [], []
    for array, rows, column in pieces:
        starts.append(starts[-1] + array.shape[0])
        rows_at += rows
        columns_at += [column] * array.shape[0]
    height, width = pieces[0][0].shape[1:]

    def source_spec(start, count):
        return pl.BlockSpec(
            (1, height, width),
            lambda step, rows, columns: (jnp.clip(step - start, 0, count - 1), 0, 0),
        )

    return pl.pallas_call(
        partial(place_kernel, tuple(starts)),
        grid_spec=pltpu.PrefetchScalarGridSpec(
            num_scalar_prefetch=2,
            grid=(starts[-1],),
            in_specs=[source_spec(start, piece[0].shape[0]) for start, piece in zip(starts, pieces)],
            out_specs=pl.BlockSpec(
                (1, height, width), lambda step, rows, columns: (rows[step], 0, columns[step])
            ),
        ),
        out_shape=jax.ShapeDtypeStruct((row_blocks, height, width * column_blocks), dtype),
    )(
        jnp.stack([jnp.asarray(r, jnp.int32) for r in rows_at]),
        jnp.stack([jnp.asarray(c, jnp.int32) for c in columns_at]),
        *[piece[0] for piece in pieces],
    )


def gather_rows(row, column, dp_count, fsdp_count, shard):
    height, width = shard.shape
    quarters = shard.reshape(4, height // 4, width)
    part = row & 3
    mine = lax.dynamic_slice_in_dim(quarters, part, 1)
    fetched = [(0, mine)]
    for bit in range(bits_of(fsdp_count)):
        fetched += [(mask | 1 << bit, swap(a, "fsdp", fsdp_count, bit)) for mask, a in fetched]
    shared = [(mask, 0, a) for mask, a in fetched[1:]]
    for bit in (1, 0):
        shared += [(mask, at | 1 << bit, swap(a, "dp", dp_count, bit)) for mask, at, a in shared]
    pieces = [(quarters, [column * 4 + i for i in range(4)], 0)]
    pieces += [(a, [(column ^ mask) * 4 + (part ^ at)], 0) for mask, at, a in shared]
    return place(pieces, fsdp_count * 4, 1, shard.dtype).reshape(fsdp_count * height, width)


def gather_small(column, fsdp_count, shards):
    packed = jnp.concatenate([shard.reshape(-1) for shard in shards])
    fetched = [packed]
    for bit in range(bits_of(fsdp_count)):
        fetched += [swap(a, "fsdp", fsdp_count, bit) for a in fetched]
    whole = jnp.stack(fetched)
    for bit in range(bits_of(fsdp_count)):
        pairs = whole.reshape(-1, 2, 1 << bit, packed.shape[0])
        whole = jnp.where((column >> bit) & 1 == 1, pairs[:, ::-1], pairs)
    whole = whole.reshape(fsdp_count, -1)
    results, start = [], 0
    for shard in shards:
        stop = start + shard.size
        results.append(whole[:, start:stop].reshape((-1,) + shard.shape[1:]))
        start = stop
    return results


def halves(values, bit_value):
    pairs = values.reshape(2, values.shape[0] // 2, values.shape[1])
    return (
        lax.dynamic_index_in_dim(pairs, 1 - bit_value, 0, False),
        lax.dynamic_index_in_dim(pairs, bit_value, 0, False),
    )


def halve(keep, received, axis, index, count, bit):
    send, kept = halves(keep.astype(jnp.float32) + received.astype(jnp.float32), (index >> bit) & 1)
    return kept.astype(jnp.bfloat16), swap(send.astype(jnp.bfloat16), axis, count, bit)


def reduce_product(row, column, dp_count, fsdp_count, former, latter):
    width = latter.shape[1] // 2
    core = row & 1
    send_columns = lax.dynamic_slice_in_dim(latter, (1 - core) * width, width, 1)
    keep_columns = lax.dynamic_slice_in_dim(latter, core * width, width, 1)
    received = swap(rows_product(former, send_columns).astype(jnp.bfloat16), "dp", dp_count, 0)
    keep = rows_product(former, keep_columns)
    for bit in reversed(range(bits_of(fsdp_count))):
        keep, received = halve(keep, received, "fsdp", column, fsdp_count, bit)
    dp_bits = bits_of(dp_count)
    for bit in range(1, dp_bits - 1):
        keep, received = halve(keep, received, "dp", row, dp_count, bit)
    share = lax.reduce_precision(keep.astype(jnp.float32) + received.astype(jnp.float32), 8, 7)
    received = swap(share.astype(jnp.bfloat16), "dp", dp_count, dp_bits - 1)
    share = (share + received.astype(jnp.float32)).astype(jnp.bfloat16)
    blocks = [(0, 0, share[None])]
    for bit in reversed(range(1, dp_bits - 1)):
        mask = 1 << (dp_bits - 2 - bit)
        blocks += [(at | mask, 0, swap(a, "dp", dp_count, bit)) for at, _, a in blocks]
    blocks += [(at, 1, swap(a, "dp", dp_count, 0)) for at, _, a in blocks]
    here = 0
    for bit in range(1, dp_bits - 1):
        here = here * 2 + ((row >> bit) & 1)
    pieces = [(a, [here ^ at], core ^ other) for at, other, a in blocks]
    total = place(pieces, 1 << (dp_bits - 2), 2, jnp.float32)
    return total.reshape(-1, width * 2)


def reduce_small(column, dp_count, fsdp_count, parts):
    packed = jnp.concatenate([part.reshape(-1) for part in parts])
    for bit in range(bits_of(fsdp_count)):
        packed = packed + swap(packed, "fsdp", fsdp_count, bit)
    for bit in range(bits_of(dp_count)):
        packed = packed + swap(packed, "dp", dp_count, bit)
    results, start = [], 0
    for part in parts:
        stop = start + part.size
        shards = packed[start:stop].reshape((fsdp_count, part.shape[0] // fsdp_count) + part.shape[1:])
        results.append(lax.dynamic_index_in_dim(shards, column, 0, False))
        start = stop
    return results


def local(
    dp_count,
    fsdp_count,
    tokens,
    cotangent,
    segments,
    bucket_line,
    bucket_plane,
    query_weight,
    query_bias,
    key_weight,
    value_weight,
    value_bias,
    output_weight,
    output_bias,
    attn_gain,
    attn_shift,
    inner_weight,
    inner_bias,
    outer_weight,
    outer_bias,
    ffn_gain,
    ffn_shift,
    line_table,
    plane_table,
):
    row = lax.axis_index("dp")
    column = lax.axis_index("fsdp")
    spread = partial(gather_rows, row, column, dp_count, fsdp_count)
    gather_total = partial(reduce_product, row, column, dp_count, fsdp_count)
    (
        b_query,
        b_values,
        b_output,
        g_attn,
        s_attn,
        b_inner,
        b_outer,
        g_ffn,
        s_ffn,
        t_line,
        t_plane,
    ) = gather_small(
        column,
        fsdp_count,
        (
            query_bias,
            value_bias,
            output_bias,
            attn_gain,
            attn_shift,
            inner_bias,
            outer_bias,
            ffn_gain,
            ffn_shift,
            line_table,
            plane_table,
        ),
    )
    w_query = spread(query_weight)
    w_keys = spread(key_weight)
    w_values = spread(value_weight)
    w_output = spread(output_weight)
    w_inner = spread(inner_weight)
    w_outer = spread(outer_weight)
    windows, length = segments.shape
    features = tokens.shape[1]
    row_count = tokens.shape[0]
    query = ((matmul(tokens, w_query) + b_query) * 0.125).astype(jnp.bfloat16)
    keys = matmul(tokens, w_keys).astype(jnp.bfloat16)
    values = (matmul(tokens, w_values) + b_values).astype(jnp.bfloat16)
    line_heads = t_line.T
    plane_heads = t_plane.T
    context, log_total = lax.map(
        partial(window_forward, line_heads, plane_heads),
        (
            query.reshape(windows, length, features),
            keys.reshape(windows, length, features),
            values.reshape(windows, length, features),
            segments,
            bucket_line,
            bucket_plane,
        ),
    )
    context_low = context.reshape(row_count, features).astype(jnp.bfloat16)
    attended = matmul(context_low, w_output) + b_output
    mid = tokens.astype(jnp.float32) + attended
    first, first_back = jax.vjp(
        layer_norm, mid, g_attn.astype(jnp.float32), s_attn.astype(jnp.float32)
    )
    first_low = first.astype(jnp.bfloat16)
    inner = matmul(first_low, w_inner) + b_inner
    activated, gelu_back = jax.vjp(partial(jax.nn.gelu, approximate=False), inner)
    activated_low = activated.astype(jnp.bfloat16)
    outer = matmul(activated_low, w_outer) + b_outer
    result, second_back = jax.vjp(
        layer_norm, first + outer, g_ffn.astype(jnp.float32), s_ffn.astype(jnp.float32)
    )
    layer_out = result.astype(jnp.bfloat16)
    dsum, grad_ffn_gain, grad_ffn_shift = second_back(cotangent.astype(jnp.float32))
    douter = dsum.astype(jnp.bfloat16)
    grad_outer_weight = gather_total(activated_low, douter)
    grad_outer_bias = jnp.sum(douter.astype(jnp.float32), 0)
    (dinner_full,) = gelu_back(back_product(douter, w_outer))
    dinner = dinner_full.astype(jnp.bfloat16)
    grad_inner_weight = gather_total(first_low, dinner)
    grad_inner_bias = jnp.sum(dinner.astype(jnp.float32), 0)
    dfirst = back_product(dinner, w_inner) + dsum
    dmid, grad_attn_gain, grad_attn_shift = first_back(dfirst)
    dattended = dmid.astype(jnp.bfloat16)
    grad_output_weight = gather_total(context_low, dattended)
    grad_output_bias = jnp.sum(dattended.astype(jnp.float32), 0)
    dcontext = back_product(dattended, w_output).astype(jnp.bfloat16)
    dquery, dkeys, dvalues, line_grads, plane_grads = lax.map(
        partial(window_backward, t_line.T, t_plane.T),
        (
            query.reshape(windows, length, features),
            keys.reshape(windows, length, features),
            values.reshape(windows, length, features),
            segments,
            bucket_line,
            bucket_plane,
            log_total,
            dcontext.reshape(windows, length, features),
        ),
    )
    dquery_low = dquery.reshape(row_count, features).astype(jnp.bfloat16) * 0.125
    dkeys_low = dkeys.reshape(row_count, features).astype(jnp.bfloat16)
    dvalues_low = dvalues.reshape(row_count, features).astype(jnp.bfloat16)
    grad_query_weight = gather_total(tokens, dquery_low)
    grad_query_bias = jnp.sum(dquery_low.astype(jnp.float32), 0)
    grad_key_weight = gather_total(tokens, dkeys_low)
    grad_value_weight = gather_total(tokens, dvalues_low)
    grad_value_bias = jnp.sum(dvalues_low.astype(jnp.float32), 0)
    grad_line_table = jnp.sum(line_grads, 0).T
    grad_plane_table = jnp.sum(plane_grads, 0).T
    input_grad = (
        dmid
        + back_product(dquery_low, w_query)
        + back_product(dkeys_low, w_keys)
        + back_product(dvalues_low, w_values)
    )
    (
        grad_query_bias,
        grad_value_bias,
        grad_output_bias,
        grad_attn_gain,
        grad_attn_shift,
        grad_inner_bias,
        grad_outer_bias,
        grad_ffn_gain,
        grad_ffn_shift,
        grad_line_table,
        grad_plane_table,
    ) = reduce_small(
        column,
        dp_count,
        fsdp_count,
        (
            grad_query_bias,
            grad_value_bias,
            grad_output_bias,
            grad_attn_gain,
            grad_attn_shift,
            grad_inner_bias,
            grad_outer_bias,
            grad_ffn_gain,
            grad_ffn_shift,
            grad_line_table,
            grad_plane_table,
        ),
    )
    return (
        layer_out,
        input_grad,
        grad_query_weight,
        grad_query_bias,
        grad_key_weight,
        grad_value_weight,
        grad_value_bias,
        grad_output_weight,
        grad_output_bias,
        grad_attn_gain,
        grad_attn_shift,
        grad_inner_weight,
        grad_inner_bias,
        grad_outer_weight,
        grad_outer_bias,
        grad_ffn_gain,
        grad_ffn_shift,
        grad_line_table,
        grad_plane_table,
    )


def solution(mesh):
    in_specs = (
        P(("dp", "fsdp"), None),
        P(("dp", "fsdp"), None),
        P(("dp", "fsdp"), None),
        P(("dp", "fsdp"), None, None),
        P(("dp", "fsdp"), None, None),
        P("fsdp", None),
        P("fsdp"),
        P("fsdp", None),
        P("fsdp", None),
        P("fsdp"),
        P("fsdp", None),
        P("fsdp"),
        P("fsdp"),
        P("fsdp"),
        P("fsdp", None),
        P("fsdp"),
        P("fsdp", None),
        P("fsdp"),
        P("fsdp"),
        P("fsdp"),
        P("fsdp", None),
        P("fsdp", None),
    )
    out_specs = (
        P(("dp", "fsdp"), None),
        P(("dp", "fsdp"), None),
        P("fsdp", None),
        P("fsdp"),
        P("fsdp", None),
        P("fsdp", None),
        P("fsdp"),
        P("fsdp", None),
        P("fsdp"),
        P("fsdp"),
        P("fsdp"),
        P("fsdp", None),
        P("fsdp"),
        P("fsdp", None),
        P("fsdp"),
        P("fsdp"),
        P("fsdp"),
        P("fsdp", None),
        P("fsdp", None),
    )
    body = partial(local, mesh.shape["dp"], mesh.shape["fsdp"])
    return jax.shard_map(body, mesh=mesh, in_specs=in_specs, out_specs=out_specs, check_vma=False)
```

```python
from functools import partial

import jax
import jax.numpy as jnp
from jax import lax
from jax.experimental import pallas as pl
from jax.experimental.pallas import tpu as pltpu
from jax.sharding import PartitionSpec as P

masked_score = -1000000000.0
norm_epsilon = 1e-05


def matmul(former, latter):
    return jnp.dot(former, latter, preferred_element_type=jnp.float32)


def rows_product(former, latter):
    return lax.dot_general(
        former, latter, (((0,), (0,)), ((), ())), preferred_element_type=jnp.float32
    )


def back_product(former, latter):
    return lax.dot_general(
        former, latter, (((1,), (1,)), ((), ())), preferred_element_type=jnp.float32
    )


def layer_norm(values, gain, shift):
    center = values - jnp.mean(values, -1, keepdims=True)
    spread = jnp.mean(center * center, -1, keepdims=True)
    return center * lax.rsqrt(spread + norm_epsilon) * gain + shift


def bucket_hits(bucket_rows, bucket_count):
    labels = lax.broadcasted_iota(jnp.int32, (bucket_count, 1), 0)
    return (bucket_rows.reshape(1, -1) == labels).astype(jnp.bfloat16)


def pair_grad(dscore_rows, line_rows, plane_rows, bucket_count):
    flat_grad = dscore_rows.reshape(dscore_rows.shape[0], -1)
    return (
        back_product(flat_grad, bucket_hits(line_rows, bucket_count)),
        back_product(flat_grad, bucket_hits(plane_rows, bucket_count)),
    )


def last_product(former, latter):
    return lax.dot_general(
        former, latter, (((1,), (1,)), ((), ())), preferred_element_type=jnp.float32
    )


def lane_half(shape, half):
    return (lax.broadcasted_iota(jnp.int32, shape, 1) // (shape[1] // 2)) == half


def keep_half(values, half):
    return jnp.where(lane_half(values.shape, half), values, jnp.zeros_like(values))


def attend_kernel(
    row_segment, key_segment, line, plane, tables, query, keys, values, context, weights
):
    rows, length = line.shape
    same = row_segment[...] == key_segment[...]
    pair = pl.program_id(2)
    parts = []
    for half in range(2):
        scores = last_product(keep_half(query[...], half), keys[...])
        line_row = jnp.broadcast_to(tables[0, pl.ds(pair * 2 + half, 1), :], (rows, 128))
        plane_row = jnp.broadcast_to(tables[1, pl.ds(pair * 2 + half, 1), :], (rows, 128))
        bias = []
        for start in range(0, length, 128):
            bias.append(
                jnp.take_along_axis(line_row, line[:, start : start + 128], 1)
                + jnp.take_along_axis(plane_row, plane[:, start : start + 128], 1)
            )
        scores = jnp.where(same, scores + jnp.concatenate(bias, 1), masked_score)
        expd = jnp.exp(scores - jnp.max(scores, 1, keepdims=True))
        inverse = 1.0 / jnp.sum(expd, 1, keepdims=True)
        probs = (expd * inverse).astype(jnp.bfloat16)
        weights[0, half] = probs
        parts.append(matmul(probs, values[...]))
    context[...] = jnp.where(lane_half(parts[0].shape, 0), parts[0], parts[1]).astype(jnp.bfloat16)


def attend(query, keys, values, segments, line, plane, tables, row_block=256):
    windows, length = segments.shape
    token_count, features = query.shape
    pairs = features // 128
    blocks = length // row_block
    return pl.pallas_call(
        attend_kernel,
        grid=(windows, blocks, pairs),
        in_specs=[
            pl.BlockSpec((row_block, 1), lambda w, r, p: (w * blocks + r, 0)),
            pl.BlockSpec((None, 1, length), lambda w, r, p: (w, 0, 0)),
            pl.BlockSpec((None, row_block, length), lambda w, r, p: (w, r, 0)),
            pl.BlockSpec((None, row_block, length), lambda w, r, p: (w, r, 0)),
            pl.BlockSpec(tables.shape, lambda w, r, p: (0, 0, 0)),
            pl.BlockSpec((row_block, 128), lambda w, r, p: (w * blocks + r, p)),
            pl.BlockSpec((length, 128), lambda w, r, p: (w, p)),
            pl.BlockSpec((length, 128), lambda w, r, p: (w, p)),
        ],
        out_specs=[
            pl.BlockSpec((row_block, 128), lambda w, r, p: (w * blocks + r, p)),
            pl.BlockSpec((1, 2, row_block, length), lambda w, r, p: (w, p, r, 0)),
        ],
        out_shape=[
            jax.ShapeDtypeStruct((token_count, features), jnp.bfloat16),
            jax.ShapeDtypeStruct((windows, pairs * 2, length, length), jnp.bfloat16),
        ],
        name="attend",
    )(
        segments.reshape(-1, 1),
        segments.reshape(windows, 1, length),
        line,
        plane,
        tables,
        query,
        keys,
        values,
    )


def attend_back_kernel(
    weights, dcontext, query, keys, values, dscores, dquery, dkeys, dvalues, key_total, value_total
):
    step = pl.program_id(2)

    @pl.when(step == 0)
    def _():
        key_total[...] = jnp.zeros_like(key_total)
        value_total[...] = jnp.zeros_like(value_total)

    query_parts, key_parts, value_parts = [], [], []
    for half in range(2):
        probs_low = weights[0, half]
        probs = probs_low.astype(jnp.float32)
        dprobs = last_product(keep_half(dcontext[...], half), values[...])
        inner = jnp.sum(probs * dprobs, 1, keepdims=True)
        dscore = (probs * (dprobs - inner)).astype(jnp.bfloat16)
        dscores[0, half] = dscore
        query_parts.append(matmul(dscore, keys[...]))
        key_parts.append(rows_product(dscore, query[...]))
        value_parts.append(rows_product(probs_low, dcontext[...]))
    low = lane_half(query_parts[0].shape, 0)
    dquery[...] = jnp.where(low, query_parts[0], query_parts[1]).astype(jnp.bfloat16) * 0.125
    low = lane_half(key_parts[0].shape, 0)
    key_total[...] += jnp.where(low, key_parts[0], key_parts[1])
    value_total[...] += jnp.where(low, value_parts[0], value_parts[1])

    @pl.when(step == pl.num_programs(2) - 1)
    def _():
        dkeys[...] = key_total[...].astype(jnp.bfloat16)
        dvalues[...] = value_total[...].astype(jnp.bfloat16)


def attend_back(weights, dcontext, query, keys, values, row_block=512):
    windows, heads, length, _ = weights.shape
    features = query.shape[1]
    blocks = length // row_block
    rows_spec = pl.BlockSpec((row_block, 128), lambda w, p, r: (w * blocks + r, p))
    keys_spec = pl.BlockSpec((length, 128), lambda w, p, r: (w, p))
    pairs_spec = pl.BlockSpec((1, 2, row_block, length), lambda w, p, r: (w, p, r, 0))
    tokens_type = jax.ShapeDtypeStruct(query.shape, jnp.bfloat16)
    return pl.pallas_call(
        attend_back_kernel,
        grid=(windows, heads // 2, blocks),
        in_specs=[pairs_spec, rows_spec, rows_spec, keys_spec, keys_spec],
        out_specs=[pairs_spec, rows_spec, keys_spec, keys_spec],
        out_shape=[
            jax.ShapeDtypeStruct(weights.shape, jnp.bfloat16),
            tokens_type,
            tokens_type,
            tokens_type,
        ],
        scratch_shapes=[pltpu.VMEM((length, 128), jnp.float32)] * 2,
        name="attend_back",
    )(weights, dcontext, query, keys, values)


def bits_of(count):
    return count.bit_length() - 1


def swap(value, axis, count, bit):
    return lax.ppermute(value, axis, [(i, i ^ (1 << bit)) for i in range(count)])


def place_kernel(counts, rows_at, columns_at, *refs):
    sources, out_ref = refs[:-1], refs[-1]
    step = 0
    for source, count in zip(sources, counts):
        width = source.shape[2]
        for i in range(count):
            lanes = pl.ds(pl.multiple_of(columns_at[step] * width, width), width)
            if width == out_ref.shape[2]:
                lanes = slice(None)
            out_ref[rows_at[step], :, lanes] = source[i].astype(out_ref.dtype)
            step += 1


def place(pieces, row_blocks, column_blocks, dtype):
    rows_at, columns_at = [], []
    for array, rows, column in pieces:
        rows_at += rows
        columns_at += [column] * array.shape[0]
    height, width = pieces[0][0].shape[1:]
    return pl.pallas_call(
        partial(place_kernel, [piece[0].shape[0] for piece in pieces]),
        in_specs=[pl.BlockSpec(memory_space=pltpu.SMEM)] * 2
        + [pl.BlockSpec(memory_space=pltpu.VMEM)] * len(pieces),
        out_specs=pl.BlockSpec(memory_space=pltpu.VMEM),
        out_shape=jax.ShapeDtypeStruct((row_blocks, height, width * column_blocks), dtype),
        name="place",
    )(
        jnp.stack([jnp.asarray(r, jnp.int32) for r in rows_at]),
        jnp.stack([jnp.asarray(c, jnp.int32) for c in columns_at]),
        *[piece[0] for piece in pieces],
    )


def gather_rows(row, column, dp_count, fsdp_count, shard):
    height, width = shard.shape
    quarters = shard.reshape(4, height // 4, width)
    part = row & 3
    mine = lax.dynamic_slice_in_dim(quarters, part, 1)
    fetched = [(0, mine)]
    for bit in range(bits_of(fsdp_count)):
        fetched += [(mask | 1 << bit, swap(a, "fsdp", fsdp_count, bit)) for mask, a in fetched]
    shared = [(mask, 0, a) for mask, a in fetched[1:]]
    for bit in (1, 0):
        shared += [(mask, at | 1 << bit, swap(a, "dp", dp_count, bit)) for mask, at, a in shared]
    pieces = [(quarters, [column * 4 + i for i in range(4)], 0)]
    pieces += [(a, [(column ^ mask) * 4 + (part ^ at)], 0) for mask, at, a in shared]
    return place(pieces, fsdp_count * 4, 1, shard.dtype).reshape(fsdp_count * height, width)


def gather_small(column, fsdp_count, shards):
    packed = jnp.concatenate([shard.reshape(-1) for shard in shards])
    fetched = [packed]
    for bit in range(bits_of(fsdp_count)):
        fetched += [swap(a, "fsdp", fsdp_count, bit) for a in fetched]
    whole = jnp.stack(fetched)
    for bit in range(bits_of(fsdp_count)):
        pairs = whole.reshape(-1, 2, 1 << bit, packed.shape[0])
        whole = jnp.where((column >> bit) & 1 == 1, pairs[:, ::-1], pairs)
    whole = whole.reshape(fsdp_count, -1)
    results, start = [], 0
    for shard in shards:
        stop = start + shard.size
        results.append(whole[:, start:stop].reshape((-1,) + shard.shape[1:]))
        start = stop
    return results


def halves(values, bit_value):
    pairs = values.reshape(2, values.shape[0] // 2, values.shape[1])
    return (
        lax.dynamic_index_in_dim(pairs, 1 - bit_value, 0, False),
        lax.dynamic_index_in_dim(pairs, bit_value, 0, False),
    )


def halve(keep, received, axis, index, count, bit):
    send, kept = halves(keep.astype(jnp.float32) + received.astype(jnp.float32), (index >> bit) & 1)
    return kept.astype(jnp.bfloat16), swap(send.astype(jnp.bfloat16), axis, count, bit)


def reduce_product(row, column, dp_count, fsdp_count, former, latter):
    width = latter.shape[1] // 2
    core = row & 1
    send_columns = lax.dynamic_slice_in_dim(latter, (1 - core) * width, width, 1)
    keep_columns = lax.dynamic_slice_in_dim(latter, core * width, width, 1)
    received = swap(rows_product(former, send_columns).astype(jnp.bfloat16), "dp", dp_count, 0)
    keep = rows_product(former, keep_columns)
    for bit in reversed(range(bits_of(fsdp_count))):
        keep, received = halve(keep, received, "fsdp", column, fsdp_count, bit)
    dp_bits = bits_of(dp_count)
    for bit in range(1, dp_bits - 1):
        keep, received = halve(keep, received, "dp", row, dp_count, bit)
    share = lax.reduce_precision(keep.astype(jnp.float32) + received.astype(jnp.float32), 8, 7)
    received = swap(share.astype(jnp.bfloat16), "dp", dp_count, dp_bits - 1)
    share = (share + received.astype(jnp.float32)).astype(jnp.bfloat16)
    blocks = [(0, 0, share[None])]
    for bit in reversed(range(1, dp_bits - 1)):
        mask = 1 << (dp_bits - 2 - bit)
        blocks += [(at | mask, 0, swap(a, "dp", dp_count, bit)) for at, _, a in blocks]
    blocks += [(at, 1, swap(a, "dp", dp_count, 0)) for at, _, a in blocks]
    here = 0
    for bit in range(1, dp_bits - 1):
        here = here * 2 + ((row >> bit) & 1)
    pieces = [(a, [here ^ at], core ^ other) for at, other, a in blocks]
    total = place(pieces, 1 << (dp_bits - 2), 2, jnp.float32)
    return total.reshape(-1, width * 2)


def reduce_small(column, dp_count, fsdp_count, parts):
    packed = jnp.concatenate([part.reshape(-1) for part in parts])
    for bit in range(bits_of(fsdp_count)):
        packed = packed + swap(packed, "fsdp", fsdp_count, bit)
    for bit in range(bits_of(dp_count)):
        packed = packed + swap(packed, "dp", dp_count, bit)
    results, start = [], 0
    for part in parts:
        stop = start + part.size
        shards = packed[start:stop].reshape((fsdp_count, part.shape[0] // fsdp_count) + part.shape[1:])
        results.append(lax.dynamic_index_in_dim(shards, column, 0, False))
        start = stop
    return results


def local(
    dp_count,
    fsdp_count,
    tokens,
    cotangent,
    segments,
    bucket_line,
    bucket_plane,
    query_weight,
    query_bias,
    key_weight,
    value_weight,
    value_bias,
    output_weight,
    output_bias,
    attn_gain,
    attn_shift,
    inner_weight,
    inner_bias,
    outer_weight,
    outer_bias,
    ffn_gain,
    ffn_shift,
    line_table,
    plane_table,
):
    row = lax.axis_index("dp")
    column = lax.axis_index("fsdp")
    spread = partial(gather_rows, row, column, dp_count, fsdp_count)
    gather_total = partial(reduce_product, row, column, dp_count, fsdp_count)
    (
        b_query,
        b_values,
        b_output,
        g_attn,
        s_attn,
        b_inner,
        b_outer,
        g_ffn,
        s_ffn,
        t_line,
        t_plane,
    ) = gather_small(
        column,
        fsdp_count,
        (
            query_bias,
            value_bias,
            output_bias,
            attn_gain,
            attn_shift,
            inner_bias,
            outer_bias,
            ffn_gain,
            ffn_shift,
            line_table,
            plane_table,
        ),
    )
    w_query = spread(query_weight)
    w_keys = spread(key_weight)
    w_values = spread(value_weight)
    w_output = spread(output_weight)
    w_inner = spread(inner_weight)
    w_outer = spread(outer_weight)
    windows, length = segments.shape
    features = tokens.shape[1]
    row_count = tokens.shape[0]
    query = ((matmul(tokens, w_query) + b_query) * 0.125).astype(jnp.bfloat16)
    keys = matmul(tokens, w_keys).astype(jnp.bfloat16)
    values = (matmul(tokens, w_values) + b_values).astype(jnp.bfloat16)
    bucket_count, head_count = t_line.shape
    tables = jnp.stack([t_line.T, t_plane.T]).astype(jnp.float32)
    tables = jnp.pad(tables, ((0, 0), (0, -head_count % 8), (0, 128 - bucket_count)))
    context_low, weights = attend(query, keys, values, segments, bucket_line, bucket_plane, tables)
    attended = matmul(context_low, w_output) + b_output
    mid = tokens.astype(jnp.float32) + attended
    first, first_back = jax.vjp(
        layer_norm, mid, g_attn.astype(jnp.float32), s_attn.astype(jnp.float32)
    )
    first_low = first.astype(jnp.bfloat16)
    inner = matmul(first_low, w_inner) + b_inner
    chance = 0.5 + 0.5 * lax.erf(inner * 0.5**0.5)
    slope = chance + inner * jnp.exp(-0.5 * inner * inner) * (0.5 / jnp.pi) ** 0.5
    activated_low = (inner * chance).astype(jnp.bfloat16)
    outer = matmul(activated_low, w_outer) + b_outer
    result, second_back = jax.vjp(
        layer_norm, first + outer, g_ffn.astype(jnp.float32), s_ffn.astype(jnp.float32)
    )
    layer_out = result.astype(jnp.bfloat16)
    dsum, grad_ffn_gain, grad_ffn_shift = second_back(cotangent.astype(jnp.float32))
    douter = dsum.astype(jnp.bfloat16)
    grad_outer_weight = gather_total(activated_low, douter)
    grad_outer_bias = jnp.sum(douter.astype(jnp.float32), 0)
    dinner = (back_product(douter, w_outer) * slope).astype(jnp.bfloat16)
    grad_inner_weight = gather_total(first_low, dinner)
    grad_inner_bias = jnp.sum(dinner.astype(jnp.float32), 0)
    dfirst = back_product(dinner, w_inner) + dsum
    dmid, grad_attn_gain, grad_attn_shift = first_back(dfirst)
    dattended = dmid.astype(jnp.bfloat16)
    grad_output_weight = gather_total(context_low, dattended)
    grad_output_bias = jnp.sum(dattended.astype(jnp.float32), 0)
    dcontext = back_product(dattended, w_output).astype(jnp.bfloat16)
    dscores, dquery_low, dkeys_low, dvalues_low = attend_back(
        weights, dcontext, query, keys, values
    )
    row_block = min(length, 128)
    line_grads, plane_grads = 0.0, 0.0
    for window in range(windows):
        for start in range(0, length, row_block):
            rows = slice(start, start + row_block)
            line_part, plane_part = pair_grad(
                dscores[window, :, rows],
                bucket_line[window, rows],
                bucket_plane[window, rows],
                bucket_count,
            )
            line_grads += line_part
            plane_grads += plane_part
    grad_query_weight = gather_total(tokens, dquery_low)
    grad_query_bias = jnp.sum(dquery_low.astype(jnp.float32), 0)
    grad_key_weight = gather_total(tokens, dkeys_low)
    grad_value_weight = gather_total(tokens, dvalues_low)
    grad_value_bias = jnp.sum(dvalues_low.astype(jnp.float32), 0)
    grad_line_table = line_grads.T
    grad_plane_table = plane_grads.T
    input_grad = (
        dmid
        + back_product(dquery_low, w_query)
        + back_product(dkeys_low, w_keys)
        + back_product(dvalues_low, w_values)
    )
    (
        grad_query_bias,
        grad_value_bias,
        grad_output_bias,
        grad_attn_gain,
        grad_attn_shift,
        grad_inner_bias,
        grad_outer_bias,
        grad_ffn_gain,
        grad_ffn_shift,
        grad_line_table,
        grad_plane_table,
    ) = reduce_small(
        column,
        dp_count,
        fsdp_count,
        (
            grad_query_bias,
            grad_value_bias,
            grad_output_bias,
            grad_attn_gain,
            grad_attn_shift,
            grad_inner_bias,
            grad_outer_bias,
            grad_ffn_gain,
            grad_ffn_shift,
            grad_line_table,
            grad_plane_table,
        ),
    )
    return (
        layer_out,
        input_grad,
        grad_query_weight,
        grad_query_bias,
        grad_key_weight,
        grad_value_weight,
        grad_value_bias,
        grad_output_weight,
        grad_output_bias,
        grad_attn_gain,
        grad_attn_shift,
        grad_inner_weight,
        grad_inner_bias,
        grad_outer_weight,
        grad_outer_bias,
        grad_ffn_gain,
        grad_ffn_shift,
        grad_line_table,
        grad_plane_table,
    )


def solution(mesh):
    in_specs = (
        P(("dp", "fsdp"), None),
        P(("dp", "fsdp"), None),
        P(("dp", "fsdp"), None),
        P(("dp", "fsdp"), None, None),
        P(("dp", "fsdp"), None, None),
        P("fsdp", None),
        P("fsdp"),
        P("fsdp", None),
        P("fsdp", None),
        P("fsdp"),
        P("fsdp", None),
        P("fsdp"),
        P("fsdp"),
        P("fsdp"),
        P("fsdp", None),
        P("fsdp"),
        P("fsdp", None),
        P("fsdp"),
        P("fsdp"),
        P("fsdp"),
        P("fsdp", None),
        P("fsdp", None),
    )
    out_specs = (
        P(("dp", "fsdp"), None),
        P(("dp", "fsdp"), None),
        P("fsdp", None),
        P("fsdp"),
        P("fsdp", None),
        P("fsdp", None),
        P("fsdp"),
        P("fsdp", None),
        P("fsdp"),
        P("fsdp"),
        P("fsdp"),
        P("fsdp", None),
        P("fsdp"),
        P("fsdp", None),
        P("fsdp"),
        P("fsdp"),
        P("fsdp"),
        P("fsdp", None),
        P("fsdp", None),
    )
    body = partial(local, mesh.shape["dp"], mesh.shape["fsdp"])
    return jax.shard_map(body, mesh=mesh, in_specs=in_specs, out_specs=out_specs, check_vma=False)
```
